32 devices in a mesh: groups: 2 (over x), span: 16 (over z, y, core).
Axes of the slice: x: 2, y: 2, z: 4, core: 2. Of those that a mesh axis runs over, the one named last changes fastest.
Arguments:
- queries: bfloat16 [4096, 2560], P(('groups', 'span')), parts along dimension 0, may hold values from -6 to 6
- keys: bfloat16 [4096, 2560], P(('groups', 'span')), parts along dimension 0, may hold values from -6 to 6
- values: bfloat16 [4096, 2560], P(('groups', 'span')), parts along dimension 0, may hold values from -6 to 6
- lookback: int32 [32], P(('groups', 'span')), parts along dimension 0, may hold values from 0 to 3, as said below
- proj_weight: bfloat16 [2560, 768], replicated, may hold values from -0.125 to 0.125
- features: bfloat16 [64, 192, 256], P(('groups', 'span')), parts along dimension 0, may hold values from -0.29882812 to 0.29882812
- norm_gain: float32 [192], replicated, may hold values from 0.1 to 1.9
- conv_weight: bfloat16 [27, 192, 192], replicated, may hold values from -0.078125 to 0.078125
Outputs:
- attended: bfloat16 [4096, 2560], P(('groups', 'span')), parts along dimension 0
- decoded: bfloat16 [64, 192, 256], P(('groups', 'span')), parts along dimension 0
The draws below stay inside these ranges and needn't reach their ends.
There are 2 independent parts, one for each index of `groups`. The reference program is written for one: setup_inputs(seed, part) draws one part's arguments, and reference() takes and returns one part's arrays. A program takes and returns all parts, laid end to end along the dimension named above; an argument that names none is the same for every part. Nothing has to cross between parts.
Inputs may be any that keep to these rules, and one draw needn't show every extreme that they name: lookback[c] <= c for every span c; the last span's value is 3.
All inputs are finite; a program needn't handle non-finite values.
Results may differ from the reference program's by a relative error of at most 0.0069.
Values may be sent and summed in bfloat16 or wider, within the bound.
A program may use at most 64 MiB of HBM per device.

```python
import jax
import jax.numpy as jnp
from jax import lax

FRAMES_DEV = 2
HEAD_DIM = 128
LOOKBACK = 3
CH = 192
SIDE = 16
PLANE = 256
TOK_DEV = 128
QKV_WIDTH = 2560
PATCH_WIDTH = 768
TOKENS = 2048
FRAMES = 32
N_SPAN = 16


def draw_queries(key, part):
    return jnp.clip(jax.random.normal(jax.random.fold_in(key, 1), (TOKENS, QKV_WIDTH), jnp.float32), -6.0, 6.0).astype(jnp.bfloat16)


def draw_keys(key, part):
    return jnp.clip(jax.random.normal(jax.random.fold_in(key, 2), (TOKENS, QKV_WIDTH), jnp.float32), -6.0, 6.0).astype(jnp.bfloat16)


def draw_lookback(key, part):
    span_ids = jnp.arange(N_SPAN, dtype=jnp.int32)
    chooser = jax.random.randint(jax.random.fold_in(key, 3), (N_SPAN,), 0, 4)
    minor_reach = jax.random.randint(jax.random.fold_in(key, 4), (N_SPAN,), 0, 2)
    reach_limit = jnp.where(chooser == 0, LOOKBACK, minor_reach)
    reach_limit = jnp.where(span_ids == N_SPAN - 1, LOOKBACK, reach_limit)
    return jnp.minimum(reach_limit, span_ids).astype(jnp.int32)


def level_of(stream_key, shape, split, low, largest):
    def one(position, parts):
        heights = jax.random.uniform(jax.random.fold_in(jax.random.fold_in(stream_key, 6), position), (parts,), jnp.float32, low / len(split), largest / len(split))
        return jnp.repeat(jnp.exp(heights), shape[position] // parts).reshape((-1,) + (1,) * (len(shape) - position - 1))

    level = one(*split[0])
    for cut in split[1:]:
        level = level * one(*cut)
    return level


def noise(rng, dims, deviation, most, cuts=(), kind=jnp.bfloat16):
    gain = level_of(rng, dims, cuts, -0.22, 0.18) if cuts else 1.0
    result = jax.random.normal(rng, dims, jnp.float32) * deviation * gain
    return jnp.minimum(jnp.maximum(result, -most), most).astype(kind)


def setup_inputs(seed: int = 0, part: int = 0) -> dict:
    streams_of = jax.random.split(jax.random.key(seed), 9)
    own_keys = jax.random.split(jax.random.fold_in(streams_of[8], part), 9)
    queries = draw_queries(jax.random.fold_in(jax.random.fold_in(streams_of[8], part), 71), part)
    keys = draw_keys(jax.random.fold_in(jax.random.fold_in(streams_of[8], part), 71), part)
    values = noise(own_keys[2], (TOKENS, QKV_WIDTH), 1.0, 6.0, ((0, 16),))
    lookback = draw_lookback(jax.random.fold_in(jax.random.fold_in(streams_of[8], part), 71), part)
    proj_weight = noise(streams_of[4], (QKV_WIDTH, PATCH_WIDTH), QKV_WIDTH ** -0.5, 0.125)
    features = noise(own_keys[5], (FRAMES, CH, PLANE), 0.05, 0.29882812, ((0, 16),))
    norm_gain = jnp.clip(1.0 + 0.18 * jax.random.normal(streams_of[6], (CH,), jnp.float32), 0.1, 1.9)
    conv_weight = noise(streams_of[7], (27, CH, CH), (27 * CH) ** -0.5, 0.078125)
    return {"queries": queries, "keys": keys, "values": values, "lookback": lookback, "proj_weight": proj_weight, "features": features, "norm_gain": norm_gain, "conv_weight": conv_weight}


eps = 1e-06

def attend(query_rows, key_rows, value_rows, reach_limit):
    row_count = query_rows.shape[0]
    head_count = query_rows.shape[1] // HEAD_DIM
    query_heads = query_rows.astype(jnp.float32).reshape(row_count, head_count, HEAD_DIM)
    key_heads = key_rows.astype(jnp.float32).reshape(key_rows.shape[0], head_count, HEAD_DIM)
    value_heads = value_rows.astype(jnp.float32).reshape(value_rows.shape[0], head_count, HEAD_DIM)
    scores = jnp.einsum('thd,khd->htk', query_heads, key_heads) * HEAD_DIM ** (-0.5)
    distance = jnp.repeat(jnp.arange(LOOKBACK + 1, dtype=jnp.int32), TOK_DEV)
    usable = distance <= reach_limit
    scores = jnp.where(usable[None, None, :], scores, -jnp.inf)
    row_max = lax.optimization_barrier(jnp.max(scores, axis=2, keepdims=True))
    weights = jnp.exp(scores - row_max)
    row_total = lax.optimization_barrier(jnp.sum(weights, axis=2))
    rounded = lax.optimization_barrier(weights.astype(jnp.bfloat16)).astype(jnp.float32)
    blended = jnp.einsum('htk,khd->thd', rounded, value_heads)
    return (blended / row_total.T[:, :, None]).reshape(row_count, -1).astype(jnp.bfloat16)

def unpatch(projected, frame_count, channels):
    shaped = projected.reshape(frame_count, SIDE // 2, SIDE // 2, channels, 2, 2)
    shaped = shaped.transpose(0, 3, 1, 4, 2, 5)
    return shaped.reshape(frame_count, channels, SIDE * SIDE)

def activate(frames_in, norm_gain):
    data = frames_in.astype(jnp.float32)
    mean_square = lax.optimization_barrier(jnp.mean(data * data, axis=1, keepdims=True))
    normed = data * lax.rsqrt(mean_square + eps) * norm_gain.astype(jnp.float32)[None, :, None]
    return jax.nn.silu(normed).astype(jnp.bfloat16)

def convolve(conv_input, conv_weight):
    frame_count = conv_input.shape[0] - 2
    plane_size = SIDE * SIDE
    padded = jnp.pad(conv_input, ((0, 0), (0, 0), (SIDE + 1, SIDE + 1)))
    column = jnp.arange(plane_size, dtype=jnp.int32) % SIDE
    summed = jnp.zeros((frame_count, conv_weight.shape[1], plane_size), jnp.float32)
    for lag_t in range(3):
        for lag_y in range(3):
            for lag_x in range(3):
                offset = SIDE + 1 + (lag_y - 1) * SIDE + (lag_x - 1)
                window = padded[lag_t:lag_t + frame_count, :, offset:offset + plane_size]
                inside = (column + lag_x - 1 >= 0) & (column + lag_x - 1 < SIDE)
                window = jnp.where(inside[None, None, :], window, jnp.zeros_like(window))
                tap_matrix = conv_weight[lag_t * 9 + lag_y * 3 + lag_x].astype(jnp.float32)
                summed = summed + jnp.einsum('oc,fcp->fop', tap_matrix, window.astype(jnp.float32))
    return summed

def reference(queries, keys, values, lookback, proj_weight, features, norm_gain, conv_weight):

    def one_span(span_index):
        first_row = (span_index * TOK_DEV).astype(jnp.int32)
        query_rows = lax.dynamic_slice_in_dim(queries, first_row, TOK_DEV, 0)
        key_parts = []
        value_parts = []
        for distance in range(LOOKBACK + 1):
            source_row = (jnp.maximum(span_index - distance, 0) * TOK_DEV).astype(jnp.int32)
            key_parts.append(lax.dynamic_slice_in_dim(keys, source_row, TOK_DEV, 0))
            value_parts.append(lax.dynamic_slice_in_dim(values, source_row, TOK_DEV, 0))
        return attend(query_rows, jnp.concatenate(key_parts, axis=0), jnp.concatenate(value_parts, axis=0), lookback[span_index])
    span_ids = jnp.arange(N_SPAN, dtype=jnp.int32)
    attended = lax.map(one_span, span_ids).reshape(TOKENS, -1)
    projected = jnp.dot(attended, proj_weight, preferred_element_type=jnp.float32)
    latent = (features.astype(jnp.float32) + unpatch(projected, FRAMES, CH)).astype(jnp.bfloat16)
    activated = activate(latent, norm_gain)
    padded_frames = jnp.concatenate([jnp.zeros((2,) + activated.shape[1:], jnp.bfloat16), activated], axis=0)

    def one_block(span_index):
        first_frame = (span_index * FRAMES_DEV).astype(jnp.int32)
        conv_input = lax.dynamic_slice_in_dim(padded_frames, first_frame, FRAMES_DEV + 2, 0)
        frames_in = lax.dynamic_slice_in_dim(latent, first_frame, FRAMES_DEV, 0)
        return (frames_in.astype(jnp.float32) + convolve(conv_input, conv_weight)).astype(jnp.bfloat16)
    decoded = lax.map(one_block, span_ids).reshape(FRAMES, CH, SIDE * SIDE)
    return (attended, decoded)
```

```python
import functools

import jax
import jax.numpy as jnp
from jax import lax
from jax.experimental import pallas as pl
from jax.experimental.pallas import tpu as pltpu
from jax.sharding import PartitionSpec as P

HEAD_DIM = 128
LOOKBACK = 3
SIDE = 16
PLANE = SIDE * SIDE
HEADS_PER_CHUNK = 2
CHUNK = HEADS_PER_CHUNK * HEAD_DIM
AHEAD = 4
MESH = pl.DeviceIdType.MESH
F32 = jnp.float32
BF16 = jnp.bfloat16

eps = 1e-06

PARTNERS = ((1, 2, -3, -1), (2, 3, 4, -1, 1, -4), (1, -1, -2, -3), (3, -1, -2, 1))
OWN, NEAR, MID, FAR, TRANSIT = range(5)


def kernel(
    n_span,
    look_ref,
    gain_ref,
    q_hbm,
    k_hbm,
    v_hbm,
    w_hbm,
    feat_hbm,
    cw_hbm,
    attb,
    decb,
    kv,
    qbuf,
    wbuf,
    fbuf,
    cwbuf,
    pacc,
    turned,
    sel,
    gain_col,
    act,
    halo,
    acc,
    wcat,
    col,
    own_sem,
    in_sem,
    ssem,
    rsem,
    hs_sem,
    hr_sem,
):
    width = qbuf.shape[1]
    chunks = width // CHUNK
    frames, channels = fbuf.shape[0], fbuf.shape[1]
    me = lax.axis_index("span")
    role = lax.rem(me, 4)
    has_prev = me >= 4
    has_next = me < n_span - 4

    def cols(j):
        return pl.ds(pl.multiple_of(j * CHUNK, CHUNK), CHUNK)

    def own_load(j, which):
        src = (k_hbm, v_hbm)[which]
        return pltpu.make_async_copy(src.at[:, cols(j)], kv.at[OWN, j, which], own_sem.at[which, j])

    def start_loads(j, carry):
        own_load(j, 0).start()
        own_load(j, 1).start()
        return carry

    lax.fori_loop(0, chunks, start_loads, 0)
    loads = [
        pltpu.make_async_copy(src, dst, in_sem.at[i])
        for i, (src, dst) in enumerate(((q_hbm, qbuf), (w_hbm, wbuf), (feat_hbm, fbuf), (cw_hbm, cwbuf)))
    ]
    loads[0].start()

    barrier = pltpu.get_barrier_semaphore()
    for kind in range(4):
        for offset in PARTNERS[kind]:
            other = me + offset

            @pl.when((role == kind) & (other >= 0) & (other < n_span))
            def _(other=other):
                pl.semaphore_signal(barrier, inc=1, device_id={"span": other}, device_id_type=MESH)

    greeted = jnp.int32(0)
    for kind in range(4):
        for offset in PARTNERS[kind]:
            other = me + offset
            greeted += ((role == kind) & (other >= 0) & (other < n_span)).astype(jnp.int32)
    pl.semaphore_wait(barrier, greeted)

    def copy(flow, src, dst, j, offset):
        return pltpu.make_async_remote_copy(
            src_ref=kv.at[src, j],
            dst_ref=kv.at[dst, j],
            send_sem=ssem.at[flow],
            recv_sem=rsem.at[dst, j],
            device_id={"span": me + offset},
            device_id_type=MESH,
        )

    def arrived(slot, j, offset):
        copy(0, slot, slot, j, offset).wait_recv()

    a0, a1, b0, b1 = (role == kind for kind in range(4))

    own_flows = (
        (a0, 0, OWN, MID, 2),
        (a0, 1, OWN, NEAR, 1),
        (a1, 0, OWN, MID, 2),
        (a1 & has_next, 1, OWN, FAR, 3),
        (b0 & has_next, 0, OWN, TRANSIT, -1),
        (b0, 1, OWN, NEAR, 1),
        (b1 & has_next, 0, OWN, FAR, 3),
    )
    early_relays = (
        (a1 & has_next, 2, TRANSIT, FAR, 4),
        (b0 & has_prev, 2, FAR, NEAR, -2),
    )
    first_relays = (
        (b0, 3, MID, FAR, 1),
        (b1, 1, MID, NEAR, -1),
    )
    second_relays = (
        (a0 & has_prev, 2, NEAR, MID, 1),
        (a1 & has_prev, 3, FAR, MID, -1),
    )
    arrivals = (
        (a0 & has_prev, MID),
        (a0 & has_prev, FAR),
        (a1, NEAR),
        (a1 & has_prev, MID),
        (b0, NEAR),
        (b1, NEAR),
        (b1, FAR),
    )

    def send_own(j):
        own_load(j, 0).wait()
        own_load(j, 1).wait()
        for cond, flow, src, dst, offset in own_flows:

            @pl.when(cond)
            def _(flow=flow, src=src, dst=dst, offset=offset):
                copy(flow, src, dst, j, offset).start()

    def pass_on(relays, j):
        for cond, flow, src, dst, offset in relays:

            @pl.when(cond)
            def _(flow=flow, src=src, dst=dst, offset=offset):
                arrived(src, j, offset)
                copy(flow, src, dst, j, offset).start()

    for j in range(AHEAD):
        send_own(jnp.int32(j))
    for load in loads[1:]:
        load.start()

    for distance in range(1, LOOKBACK + 1):

        @pl.when(me < distance)
        def _(distance=distance):
            kv[distance] = jnp.zeros(kv.shape[1:], BF16)

    pacc[...] = jnp.zeros_like(pacc)
    rows = lax.broadcasted_iota(jnp.int32, sel.shape, 0)
    places = lax.broadcasted_iota(jnp.int32, sel.shape, 1)
    pixel = places & (PLANE - 1)
    token = (places >> 8) * (PLANE // 4) + (pixel >> 5) * (SIDE // 2) + ((pixel & (SIDE - 1)) >> 1)
    corner = ((pixel >> 4) & 1) * 2 + (pixel & 1)
    hit = ((rows & 127) == token) & ((rows >> 7) == corner)
    sel[...] = jnp.where(hit, 1.0, 0.0).astype(BF16)
    square = (channels, channels)
    diagonal = lax.broadcasted_iota(jnp.int32, square, 0) == lax.broadcasted_iota(jnp.int32, square, 1)
    gain_col[...] = jnp.sum(jnp.where(diagonal, gain_ref[...], 0.0), axis=1, keepdims=True)
    distance = lax.broadcasted_iota(jnp.int32, (1, (LOOKBACK + 1) * 128), 1) >> 7
    usable = distance <= look_ref[0]

    def attend(j):
        for cond, slot in arrivals:

            @pl.when(cond)
            def _(slot=slot):
                arrived(slot, j, 0)

        for head in range(HEADS_PER_CHUNK):
            at = pl.ds(pl.multiple_of(j * CHUNK + head * HEAD_DIM, HEAD_DIM), HEAD_DIM)
            within = slice(head * HEAD_DIM, (head + 1) * HEAD_DIM)
            keys = kv[0:4, j, 0, :, within].reshape(-1, HEAD_DIM)
            values = kv[0:4, j, 1, :, within].reshape(-1, HEAD_DIM)
            scores = lax.dot_general(
                qbuf[:, at], keys, (((1,), (1,)), ((), ())), preferred_element_type=F32
            ) * HEAD_DIM ** (-0.5)
            scores = jnp.where(usable, scores, -jnp.inf)
            row_max = jnp.max(scores, axis=1, keepdims=True)
            weights = jnp.exp(scores - row_max)
            row_total = jnp.sum(weights, axis=1, keepdims=True)
            blended = jnp.dot(weights.astype(BF16), values, preferred_element_type=F32)
            attb[:, at] = (blended / row_total).astype(BF16)
        pacc[...] += jnp.dot(attb[:, cols(j)], wbuf[cols(j), :], preferred_element_type=F32)

    pass_on(early_relays, jnp.int32(0))

    def turn(i, carry):
        @pl.when(i + AHEAD < chunks)
        def _():
            send_own(i + AHEAD)

        @pl.when(i + 1 < chunks)
        def _():
            pass_on(early_relays, i + 1)

        @pl.when(i == 1)
        def _():
            loads[0].wait()
            loads[1].wait()

        @pl.when(i == 2)
        def _():
            loads[3].wait()

        for lag in range(3):

            @pl.when(i == 3 + lag)
            def _(lag=lag):
                at = slice((2 - lag) * channels, (3 - lag) * channels)
                wcat[at, :] = jnp.concatenate([cwbuf[lag * 9 + place] for place in range(9)], axis=1)

        @pl.when(i >= 1)
        def _():
            attend(i - 1)

        @pl.when(i < chunks)
        def _():
            pass_on(first_relays, i)
            pass_on(second_relays, i)

        return carry

    lax.fori_loop(0, chunks + 1, turn, 0)

    loads[2].wait()
    turned[...] = pacc[...].T
    corners = [turned[pl.ds(corner, channels, stride=4), :] for corner in range(4)]
    tall = jnp.concatenate(corners, axis=1)
    high = tall.astype(BF16)
    low = (tall - high.astype(F32)).astype(BF16)
    spread = jnp.dot(high, sel[...], preferred_element_type=F32) + jnp.dot(low, sel[...], preferred_element_type=F32)

    def halo_copy(frame):
        return pltpu.make_async_remote_copy(
            src_ref=act.at[frame],
            dst_ref=halo.at[frame],
            send_sem=hs_sem.at[frame],
            recv_sem=hr_sem.at[frame],
            device_id={"span": me + 1},
            device_id_type=MESH,
        )

    for frame in range(frames):
        latent = (fbuf[frame].astype(F32) + spread[:, frame * PLANE : (frame + 1) * PLANE]).astype(BF16)
        decb[frame] = latent
        data = latent.astype(F32)
        mean_square = jnp.mean(data * data, axis=0, keepdims=True)
        normed = data * lax.rsqrt(mean_square + eps) * gain_col[...]
        act[frame] = (normed / (1.0 + jnp.exp(-normed))).astype(BF16)

        @pl.when(me < n_span - 1)
        def _(frame=frame):
            halo_copy(frame).start()

    lane = lax.broadcasted_iota(jnp.int32, (1, PLANE), 1)
    line, column = lane >> 4, lane & (SIDE - 1)

    def keep(cond):
        return jnp.where(cond, 1.0, 0.0).astype(BF16)

    sides = (keep(column >= 1), None, keep(column < SIDE - 1))
    ends = (keep(line >= 1), None, keep(line < SIDE - 1))

    def shifted(data, shift, mask):
        return data if mask is None else pltpu.roll(data, shift % PLANE, 1) * mask

    def unfold(slot, data):
        for lag_x in range(3):
            across = shifted(data, 1 - lag_x, sides[lag_x])
            for lag_y in range(3):
                place = lag_y * 3 + lag_x
                col[slot, place * channels : (place + 1) * channels, :] = shifted(
                    across, (1 - lag_y) * SIDE, ends[lag_y]
                )

    def taps(slot, first, last):
        return jnp.dot(
            wcat[first * channels : last * channels, :], col[slot], preferred_element_type=F32
        )

    unfold(0, act[0])
    both = taps(0, 0, 2)
    acc[0] = both[:channels]
    unfold(1, act[1])
    acc[1] = both[channels:] + taps(1, 0, 1)

    @pl.when(me > 0)
    def _():
        halo_copy(0).wait_recv()
        unfold(0, halo[0])
        acc[0] += taps(0, 2, 3)
        halo_copy(1).wait_recv()
        unfold(1, halo[1])
        both = taps(1, 1, 3)
        acc[0] += both[:channels]
        acc[1] += both[channels:]

    for frame in range(frames):
        decb[frame] = (decb[frame].astype(F32) + acc[frame]).astype(BF16)

    @pl.when(me < n_span - 1)
    def _():
        halo_copy(0).wait_send()
        halo_copy(1).wait_send()

    for cond, flow, src, dst, offset in own_flows + early_relays + first_relays + second_relays:

        @pl.when(cond)
        def _(flow=flow, src=src, dst=dst, offset=offset):
            pltpu.make_async_remote_copy(
                src_ref=kv.at[src],
                dst_ref=kv.at[dst],
                send_sem=ssem.at[flow],
                recv_sem=rsem.at[dst, 0],
                device_id={"span": me + offset},
                device_id_type=MESH,
            ).wait_send()


def publish(att_vmem, dec_vmem, att_hbm, dec_hbm, sem):
    copies = [
        pltpu.make_async_copy(src, dst, sem.at[i])
        for i, (src, dst) in enumerate(((att_vmem, att_hbm), (dec_vmem, dec_hbm)))
    ]
    for copy in copies:
        copy.start()
    for copy in copies:
        copy.wait()


def solution(mesh):
    n_span = mesh.shape["span"]

    def shards(queries, keys, values, lookback, proj_weight, features, norm_gain, conv_weight):
        tokens, width = queries.shape
        frames, channels, plane = features.shape
        chunks = width // CHUNK
        patch = proj_weight.shape[1]
        dma = pltpu.SemaphoreType.DMA
        hbm = pl.BlockSpec(memory_space=pltpu.HBM)
        vmem = pl.BlockSpec(memory_space=pltpu.VMEM)
        attended, decoded = pl.pallas_call(
            functools.partial(kernel, n_span),
            out_shape=(
                pltpu.VMEM(queries.shape, BF16),
                pltpu.VMEM(features.shape, BF16),
            ),
            in_specs=[
                pl.BlockSpec(memory_space=pltpu.SMEM),
                pl.BlockSpec(memory_space=pltpu.VMEM),
            ]
            + [hbm] * 6,
            out_specs=(vmem, vmem),
            scratch_shapes=[
                pltpu.VMEM((5, chunks, 2, tokens, CHUNK), BF16),
                pltpu.VMEM((tokens, width), BF16),
                pltpu.VMEM(proj_weight.shape, BF16),
                pltpu.VMEM(features.shape, BF16),
                pltpu.VMEM(conv_weight.shape, BF16),
                pltpu.VMEM((tokens, patch), F32),
                pltpu.VMEM((patch, tokens), F32),
                pltpu.VMEM((4 * tokens, frames * plane), BF16),
                pltpu.VMEM((channels, 1), F32),
                pltpu.VMEM(features.shape, BF16),
                pltpu.VMEM(features.shape, BF16),
                pltpu.VMEM(features.shape, F32),
                pltpu.VMEM((3 * channels, 9 * channels), BF16),
                pltpu.VMEM((2, 9 * channels, plane), BF16),
                dma((2, chunks)),
                dma((4,)),
                dma((4,)),
                dma((5, chunks)),
                dma((2,)),
                dma((2,)),
            ],
            compiler_params=pltpu.CompilerParams(collective_id=0, has_side_effects=True),
        )(lookback, norm_gain.reshape(1, -1), queries, keys, values, proj_weight, features, conv_weight)
        return pl.pallas_call(
            publish,
            out_shape=(
                jax.ShapeDtypeStruct(queries.shape, BF16),
                jax.ShapeDtypeStruct(features.shape, BF16),
            ),
            in_specs=[vmem, vmem],
            out_specs=(hbm, hbm),
            scratch_shapes=[dma((2,))],
        )(
            pltpu.with_memory_space_constraint(attended, pltpu.VMEM),
            pltpu.with_memory_space_constraint(decoded, pltpu.VMEM),
        )

    rows = P(("groups", "span"), None)
    planes = P(("groups", "span"), None, None)
    return jax.shard_map(
        shards,
        mesh=mesh,
        in_specs=(rows, rows, rows, P(("groups", "span")), P(), planes, P(), P()),
        out_specs=(rows, planes),
        check_vma=False,
    )
```

```python
import functools

import jax
import jax.numpy as jnp
from jax import lax
from jax.experimental import pallas as pl
from jax.experimental.pallas import tpu as pltpu
from jax.sharding import PartitionSpec as P

HEAD_DIM = 128
LOOKBACK = 3
SIDE = 16
PLANE = SIDE * SIDE
HEADS_PER_CHUNK = 2
CHUNK = HEADS_PER_CHUNK * HEAD_DIM
AHEAD = 4
LOWER = 8
MESH = pl.DeviceIdType.MESH
F32 = jnp.float32
BF16 = jnp.bfloat16

eps = 1e-06

PARTNERS = ((1, 2, -3, -1), (2, 3, 4, -1, 1, -4), (1, -1, -2, -3, 4, -4), (3, -1, -2, 1))
OWN, NEAR, MID, FAR, TRANSIT = range(5)


def kernel(
    n_span,
    look_hbm,
    gain_hbm,
    q_hbm,
    k_hbm,
    v_hbm,
    w_hbm,
    feat_hbm,
    cw_hbm,
    attb,
    decb,
    kv,
    qbuf,
    wbuf,
    fbuf,
    cwbuf,
    pacc,
    turned,
    sel,
    gain_col,
    act,
    halo,
    acc,
    wcat,
    col,
    look_ref,
    gain_ref,
    part_sem,
    own_sem,
    in_sem,
    ssem,
    rsem,
    hs_sem,
    hr_sem,
):
    width = qbuf.shape[1]
    chunks = width // CHUNK
    frames, channels = fbuf.shape[0], fbuf.shape[1]
    n_rows = n_span // 4
    me = lax.axis_index("span")
    role = lax.rem(me, 4)
    has_prev = me >= 4
    has_next = me < n_span - 4

    barrier = pltpu.get_barrier_semaphore()
    for kind in range(4):
        for offset in PARTNERS[kind]:
            other = me + offset

            @pl.when((role == kind) & (other >= 0) & (other < n_span))
            def _(other=other):
                pl.semaphore_signal(barrier, inc=1, device_id={"span": other}, device_id_type=MESH)

    def cols(j):
        return pl.ds(pl.multiple_of(j * CHUNK, CHUNK), CHUNK)

    def own_load(j, which):
        src = (k_hbm, v_hbm)[which]
        return pltpu.make_async_copy(src.at[:, cols(j)], kv.at[OWN, j, which], own_sem.at[which, j])

    def start_loads(j, carry):
        own_load(j, 0).start()
        own_load(j, 1).start()
        return carry

    lax.fori_loop(0, chunks, start_loads, 0)
    loads = [
        pltpu.make_async_copy(src, dst, in_sem.at[i])
        for i, (src, dst) in enumerate(
            (
                (q_hbm, qbuf),
                (w_hbm, wbuf),
                (feat_hbm, fbuf),
                (cw_hbm, cwbuf),
                (look_hbm, look_ref),
                (gain_hbm, gain_ref),
            )
        )
    ]
    for load in loads[4:] + loads[:1]:
        load.start()

    greeted = jnp.int32(0)
    for kind in range(4):
        for offset in PARTNERS[kind]:
            other = me + offset
            greeted += ((role == kind) & (other >= 0) & (other < n_span)).astype(jnp.int32)
    pl.semaphore_wait(barrier, greeted)

    def copy(flow, src, dst, j, offset):
        return pltpu.make_async_remote_copy(
            src_ref=kv.at[src, j],
            dst_ref=kv.at[dst, j],
            send_sem=ssem.at[flow],
            recv_sem=rsem.at[dst, j],
            device_id={"span": me + offset},
            device_id_type=MESH,
        )

    def arrived(slot, j, offset):
        copy(0, slot, slot, j, offset).wait_recv()

    a0, a1, b0, b1 = (role == kind for kind in range(4))
    row = me // 4

    def crosses_below(row, j):
        share = (LOWER * chunks * (n_rows - row)) // (10 * n_rows)
        return ((j + 1) * share) // chunks > (j * share) // chunks

    def part_flows(j):
        here, before = crosses_below(row, j), crosses_below(row - 1, j)
        return (
            (b0 & has_next & here, 0, OWN, TRANSIT, -1),
            (b0 & has_next & jnp.logical_not(here), 0, OWN, TRANSIT, 4),
            (a1 & has_next & here, 0, TRANSIT, FAR, 4),
            (b0 & has_prev & jnp.logical_not(before), 1, TRANSIT, FAR, -1),
        )

    def part_copy(flow, src, dst, j, offset):
        return pltpu.make_async_remote_copy(
            src_ref=kv.at[src, j],
            dst_ref=kv.at[dst, j],
            send_sem=part_sem.at[flow, j],
            recv_sem=rsem.at[dst, j],
            device_id={"span": me + offset},
            device_id_type=MESH,
        )

    own_flows = (
        (a0, 0, OWN, MID, 2),
        (a0, 1, OWN, NEAR, 1),
        (a1, 0, OWN, MID, 2),
        (a1 & has_next, 1, OWN, FAR, 3),
        (b0, 1, OWN, NEAR, 1),
        (b1 & has_next, 0, OWN, FAR, 3),
    )
    early_relays = (
        (b0 & has_prev, 2, FAR, NEAR, -2),
    )
    first_relays = (
        (b0, 3, MID, FAR, 1),
        (b1, 1, MID, NEAR, -1),
    )
    second_relays = (
        (a0 & has_prev, 2, NEAR, MID, 1),
        (a1 & has_prev, 3, FAR, MID, -1),
    )
    arrivals = (
        (a0 & has_prev, MID),
        (a0 & has_prev, FAR),
        (a1, NEAR),
        (a1 & has_prev, MID),
        (b0, NEAR),
        (b1, NEAR),
        (b1, FAR),
    )

    def send_own(j):
        own_load(j, 0).wait()
        own_load(j, 1).wait()
        for cond, flow, src, dst, offset in own_flows:

            @pl.when(cond)
            def _(flow=flow, src=src, dst=dst, offset=offset):
                copy(flow, src, dst, j, offset).start()

        for cond, flow, src, dst, offset in part_flows(j)[:2]:

            @pl.when(cond)
            def _(flow=flow, src=src, dst=dst, offset=offset):
                part_copy(flow, src, dst, j, offset).start()

    def pass_part(j):
        for cond, flow, src, dst, offset in part_flows(j)[2:]:

            @pl.when(cond)
            def _(flow=flow, src=src, dst=dst, offset=offset):
                arrived(src, j, offset)
                part_copy(flow, src, dst, j, offset).start()

    def pass_on(relays, j):
        for cond, flow, src, dst, offset in relays:

            @pl.when(cond)
            def _(flow=flow, src=src, dst=dst, offset=offset):
                arrived(src, j, offset)
                copy(flow, src, dst, j, offset).start()

    for j in range(AHEAD):
        send_own(jnp.int32(j))
    for load in loads[1:4]:
        load.start()

    for distance in range(1, LOOKBACK + 1):

        @pl.when(me < distance)
        def _(distance=distance):
            kv[distance] = jnp.zeros(kv.shape[1:], BF16)

    pacc[...] = jnp.zeros_like(pacc)
    rows = lax.broadcasted_iota(jnp.int32, sel.shape, 0)
    places = lax.broadcasted_iota(jnp.int32, sel.shape, 1)
    pixel = places & (PLANE - 1)
    token = (places >> 8) * (PLANE // 4) + (pixel >> 5) * (SIDE // 2) + ((pixel & (SIDE - 1)) >> 1)
    corner = ((pixel >> 4) & 1) * 2 + (pixel & 1)
    hit = ((rows & 127) == token) & ((rows >> 7) == corner)
    sel[...] = jnp.where(hit, 1.0, 0.0).astype(BF16)
    square = (channels, channels)
    diagonal = lax.broadcasted_iota(jnp.int32, square, 0) == lax.broadcasted_iota(jnp.int32, square, 1)
    for load in loads[4:]:
        load.wait()
    gain_col[...] = jnp.sum(jnp.where(diagonal, gain_ref[...], 0.0), axis=1, keepdims=True)
    distance = lax.broadcasted_iota(jnp.int32, (1, (LOOKBACK + 1) * 128), 1) >> 7
    usable = distance <= look_ref[0]

    def attend(j):
        for cond, slot in arrivals:

            @pl.when(cond)
            def _(slot=slot):
                arrived(slot, j, 0)

        for head in range(HEADS_PER_CHUNK):
            at = pl.ds(pl.multiple_of(j * CHUNK + head * HEAD_DIM, HEAD_DIM), HEAD_DIM)
            within = slice(head * HEAD_DIM, (head + 1) * HEAD_DIM)
            keys = kv[0:4, j, 0, :, within].reshape(-1, HEAD_DIM)
            values = kv[0:4, j, 1, :, within].reshape(-1, HEAD_DIM)
            scores = lax.dot_general(
                qbuf[:, at], keys, (((1,), (1,)), ((), ())), preferred_element_type=F32
            ) * HEAD_DIM ** (-0.5)
            scores = jnp.where(usable, scores, -jnp.inf)
            row_max = jnp.max(scores, axis=1, keepdims=True)
            weights = jnp.exp(scores - row_max)
            row_total = jnp.sum(weights, axis=1, keepdims=True)
            blended = jnp.dot(weights.astype(BF16), values, preferred_element_type=F32)
            attb[:, at] = (blended / row_total).astype(BF16)
        pacc[...] += jnp.dot(attb[:, cols(j)], wbuf[cols(j), :], preferred_element_type=F32)

    pass_part(jnp.int32(0))
    pass_on(early_relays, jnp.int32(0))

    def turn(i, carry):
        @pl.when(i + AHEAD < chunks)
        def _():
            send_own(i + AHEAD)

        @pl.when(i + 1 < chunks)
        def _():
            pass_part(i + 1)
            pass_on(early_relays, i + 1)

        @pl.when(i == 1)
        def _():
            loads[0].wait()
            loads[1].wait()

        @pl.when(i == 2)
        def _():
            loads[3].wait()

        for lag in range(3):

            @pl.when(i == 3 + lag)
            def _(lag=lag):
                at = slice((2 - lag) * channels, (3 - lag) * channels)
                wcat[at, :] = jnp.concatenate([cwbuf[lag * 9 + place] for place in range(9)], axis=1)

        @pl.when(i >= 1)
        def _():
            attend(i - 1)

        @pl.when(i < chunks)
        def _():
            pass_on(first_relays, i)
            pass_on(second_relays, i)

        return carry

    lax.fori_loop(0, chunks + 1, turn, 0)

    loads[2].wait()
    turned[...] = pacc[...].T
    corners = [turned[pl.ds(corner, channels, stride=4), :] for corner in range(4)]
    tall = jnp.concatenate(corners, axis=1)
    high = tall.astype(BF16)
    low = (tall - high.astype(F32)).astype(BF16)
    spread = jnp.dot(high, sel[...], preferred_element_type=F32) + jnp.dot(low, sel[...], preferred_element_type=F32)

    def halo_copy(frame):
        return pltpu.make_async_remote_copy(
            src_ref=act.at[frame],
            dst_ref=halo.at[frame],
            send_sem=hs_sem.at[frame],
            recv_sem=hr_sem.at[frame],
            device_id={"span": me + 1},
            device_id_type=MESH,
        )

    for frame in range(frames):
        latent = (fbuf[frame].astype(F32) + spread[:, frame * PLANE : (frame + 1) * PLANE]).astype(BF16)
        decb[frame] = latent
        data = latent.astype(F32)
        mean_square = jnp.mean(data * data, axis=0, keepdims=True)
        normed = data * lax.rsqrt(mean_square + eps) * gain_col[...]
        act[frame] = (normed / (1.0 + jnp.exp(-normed))).astype(BF16)

        @pl.when(me < n_span - 1)
        def _(frame=frame):
            halo_copy(frame).start()

    lane = lax.broadcasted_iota(jnp.int32, (1, PLANE), 1)
    line, column = lane >> 4, lane & (SIDE - 1)

    def keep(cond):
        return jnp.where(cond, 1.0, 0.0).astype(BF16)

    sides = (keep(column >= 1), None, keep(column < SIDE - 1))
    ends = (keep(line >= 1), None, keep(line < SIDE - 1))

    def shifted(data, shift, mask):
        return data if mask is None else pltpu.roll(data, shift % PLANE, 1) * mask

    def unfold(slot, data):
        for lag_x in range(3):
            across = shifted(data, 1 - lag_x, sides[lag_x])
            for lag_y in range(3):
                place = lag_y * 3 + lag_x
                col[slot, place * channels : (place + 1) * channels, :] = shifted(
                    across, (1 - lag_y) * SIDE, ends[lag_y]
                )

    def taps(slot, first, last):
        return jnp.dot(
            wcat[first * channels : last * channels, :], col[slot], preferred_element_type=F32
        )

    unfold(0, act[0])
    both = taps(0, 0, 2)
    acc[0] = both[:channels]
    unfold(1, act[1])
    acc[1] = both[channels:] + taps(1, 0, 1)

    @pl.when(me > 0)
    def _():
        halo_copy(0).wait_recv()
        unfold(0, halo[0])
        acc[0] += taps(0, 2, 3)
        halo_copy(1).wait_recv()
        unfold(1, halo[1])
        both = taps(1, 1, 3)
        acc[0] += both[:channels]
        acc[1] += both[channels:]

    for frame in range(frames):
        decb[frame] = (decb[frame].astype(F32) + acc[frame]).astype(BF16)

    @pl.when(me < n_span - 1)
    def _():
        halo_copy(0).wait_send()
        halo_copy(1).wait_send()

    def finish(j, carry):
        for cond, flow, src, dst, offset in part_flows(j):

            @pl.when(cond)
            def _(flow=flow, src=src, dst=dst, offset=offset):
                part_copy(flow, src, dst, j, offset).wait_send()

        return carry

    @pl.when(a1 | b0)
    def _():
        lax.fori_loop(0, chunks, finish, 0)

    for cond, flow, src, dst, offset in own_flows + early_relays + first_relays + second_relays:

        @pl.when(cond)
        def _(flow=flow, src=src, dst=dst, offset=offset):
            pltpu.make_async_remote_copy(
                src_ref=kv.at[src],
                dst_ref=kv.at[dst],
                send_sem=ssem.at[flow],
                recv_sem=rsem.at[dst, 0],
                device_id={"span": me + offset},
                device_id_type=MESH,
            ).wait_send()


def publish(att_vmem, dec_vmem, att_hbm, dec_hbm, sem):
    copies = [
        pltpu.make_async_copy(src, dst, sem.at[i])
        for i, (src, dst) in enumerate(((att_vmem, att_hbm), (dec_vmem, dec_hbm)))
    ]
    for copy in copies:
        copy.start()
    for copy in copies:
        copy.wait()


def solution(mesh):
    n_span = mesh.shape["span"]

    def shards(queries, keys, values, lookback, proj_weight, features, norm_gain, conv_weight):
        tokens, width = queries.shape
        frames, channels, plane = features.shape
        chunks = width // CHUNK
        patch = proj_weight.shape[1]
        dma = pltpu.SemaphoreType.DMA
        hbm = pl.BlockSpec(memory_space=pltpu.HBM)
        vmem = pl.BlockSpec(memory_space=pltpu.VMEM)
        attended, decoded = pl.pallas_call(
            functools.partial(kernel, n_span),
            out_shape=(
                pltpu.VMEM(queries.shape, BF16),
                pltpu.VMEM(features.shape, BF16),
            ),
            in_specs=[hbm] * 8,
            out_specs=(vmem, vmem),
            scratch_shapes=[
                pltpu.VMEM((5, chunks, 2, tokens, CHUNK), BF16),
                pltpu.VMEM((tokens, width), BF16),
                pltpu.VMEM(proj_weight.shape, BF16),
                pltpu.VMEM(features.shape, BF16),
                pltpu.VMEM(conv_weight.shape, BF16),
                pltpu.VMEM((tokens, patch), F32),
                pltpu.VMEM((patch, tokens), F32),
                pltpu.VMEM((4 * tokens, frames * plane), BF16),
                pltpu.VMEM((channels, 1), F32),
                pltpu.VMEM(features.shape, BF16),
                pltpu.VMEM(features.shape, BF16),
                pltpu.VMEM(features.shape, F32),
                pltpu.VMEM((3 * channels, 9 * channels), BF16),
                pltpu.VMEM((2, 9 * channels, plane), BF16),
                pltpu.SMEM((1,), jnp.int32),
                pltpu.VMEM((1, channels), F32),
                dma((2, chunks)),
                dma((2, chunks)),
                dma((6,)),
                dma((4,)),
                dma((5, chunks)),
                dma((2,)),
                dma((2,)),
            ],
            compiler_params=pltpu.CompilerParams(collective_id=0, has_side_effects=True),
        )(lookback, norm_gain.reshape(1, -1), queries, keys, values, proj_weight, features, conv_weight)
        return pl.pallas_call(
            publish,
            out_shape=(
                jax.ShapeDtypeStruct(queries.shape, BF16),
                jax.ShapeDtypeStruct(features.shape, BF16),
            ),
            in_specs=[vmem, vmem],
            out_specs=(hbm, hbm),
            scratch_shapes=[dma((2,))],
        )(
            pltpu.with_memory_space_constraint(attended, pltpu.VMEM),
            pltpu.with_memory_space_constraint(decoded, pltpu.VMEM),
        )

    rows = P(("groups", "span"), None)
    planes = P(("groups", "span"), None, None)
    return jax.shard_map(
        shards,
        mesh=mesh,
        in_specs=(rows, rows, rows, P(("groups", "span")), P(), planes, P(), P()),
        out_specs=(rows, planes),
        check_vma=False,
    )
```
